256 devices in a mesh: seq: 32 (over x, y, core), dp: 8 (over z).
Axes of the slice: x: 4, y: 4, z: 8, core: 2. Of those that a mesh axis runs over, the one named last changes fastest.
Arguments:
- queries: bfloat16 [8, 16384, 2048], P('dp', 'seq'), may hold values from -5 to 5
- keys: bfloat16 [8, 16384, 2048], P('dp', 'seq'), may hold values from -5 to 5
- values: bfloat16 [8, 16384, 2048], P('dp', 'seq'), may hold values from -8 to 8
- out_weight: bfloat16 [2048, 4096], P(None, 'dp'), may hold values from -0.125 to 0.125
Outputs:
- projected: bfloat16 [8, 16384, 4096], P('dp', 'seq')
The draws below stay inside these ranges and needn't reach their ends.
All inputs are finite; a program needn't handle non-finite values.
Results may differ from the reference program's by a relative error of at most 0.0061.
Values may be sent and summed in bfloat16 or wider, within the bound.
No kernel may reach another device: no remote copies, remote signals or barrier semaphores. Data moves between devices by JAX's collectives and lax.ppermute only.
A program may use at most 192 MiB of HBM per device.

```python
import math
import jax
import jax.numpy as jnp
from jax import lax

D = 4096
HEADS = 16
CHANNEL_WIDTH = 128
SEGMENT_LENGTH = 256
LENGTH = 16384
NBLK = 64
SEQS = 8


def block_offsets(key, spread):
    offsets = jax.random.uniform(key, (SEQS, NBLK, 1, HEADS * CHANNEL_WIDTH), minval=-spread, maxval=spread)
    return jnp.broadcast_to(offsets, (SEQS, NBLK, SEGMENT_LENGTH, HEADS * CHANNEL_WIDTH)).reshape(SEQS, LENGTH, HEADS * CHANNEL_WIDTH)


def draw_queries(key, part):
    main_key = jax.random.fold_in(key, 11)
    shape = (SEQS, LENGTH, HEADS * CHANNEL_WIDTH)
    drawn = jnp.clip(jax.random.normal(main_key, shape), -4.5, 4.5)
    return drawn.astype(jnp.bfloat16)


def draw_keys(key, part):
    main_key = jax.random.fold_in(key, 22)
    offset_key = jax.random.fold_in(key, 23)
    shape = (SEQS, LENGTH, HEADS * CHANNEL_WIDTH)
    drawn = jax.random.normal(main_key, shape) + block_offsets(offset_key, 1.0)
    drawn = jnp.clip(drawn, -5.0, 5.0)
    return drawn.astype(jnp.bfloat16)


def draw_values(key, part):
    main_key = jax.random.fold_in(key, 33)
    offset_key = jax.random.fold_in(key, 34)
    shape = (SEQS, LENGTH, HEADS * CHANNEL_WIDTH)
    drawn = jnp.clip(jax.random.normal(main_key, shape), -4.0, 4.0) + block_offsets(offset_key, 2.0)
    return jnp.clip(drawn, -8.0, 8.0).astype(jnp.bfloat16)


def block_levels(rng, shape, pieces, low, high):
    gain = 1.0
    for dim, shards_of in pieces:
        draws = jax.random.uniform(jax.random.fold_in(jax.random.fold_in(rng, 6), dim), (shards_of,), jnp.float32, low / len(pieces), high / len(pieces))
        gain = gain * jnp.repeat(jnp.exp(draws), shape[dim] // shards_of).reshape((-1,) + (1,) * (len(shape) - 1 - dim))
    return gain


def scatter_about(stream_key, shape, width, bound, shards=(), held_as=jnp.bfloat16):
    level = block_levels(stream_key, shape, shards, -0.22, 0.18) if shards else 1.0
    values = jax.random.normal(stream_key, shape, jnp.float32) * width * level
    return jnp.minimum(jnp.maximum(values, -bound), bound).astype(held_as)


def setup_inputs(seed: int = 0) -> dict:
    splits = jax.random.split(jax.random.key(seed), 5)
    return {
        "queries": draw_queries(jax.random.fold_in(splits[4], 71), 0),
        "keys": draw_keys(jax.random.fold_in(splits[4], 71), 0),
        "values": draw_values(jax.random.fold_in(splits[4], 71), 0),
        "out_weight": scatter_about(splits[3], (HEADS * CHANNEL_WIDTH, D), (HEADS * CHANNEL_WIDTH) ** -0.5, 0.125, ((1, 8),)),
    }


def reference(queries, keys, values, out_weight):
    feature_width = HEADS * CHANNEL_WIDTH
    softmax_multiplier = 1.0 / math.sqrt(CHANNEL_WIDTH)
    faraway_offset_bias = math.log(SEGMENT_LENGTH)

    def block_means(tensor):
        summed = lax.optimization_barrier(jnp.mean(tensor.astype(jnp.float32).reshape(SEQS, NBLK, SEGMENT_LENGTH, feature_width), axis=2))
        rounded = lax.optimization_barrier(summed.astype(jnp.bfloat16))
        return rounded.astype(jnp.float32).reshape(SEQS, NBLK, HEADS, CHANNEL_WIDTH)
    span_address_means = block_means(keys)
    value_means = block_means(values)
    padding = jnp.zeros((SEQS, SEGMENT_LENGTH, feature_width), keys.dtype)
    keys_padded = jnp.concatenate([padding, keys], axis=1)
    values_padded = jnp.concatenate([padding, values], axis=1)
    query_pos = jnp.arange(SEGMENT_LENGTH, dtype=jnp.int32)
    key_pos = jnp.arange(2 * SEGMENT_LENGTH, dtype=jnp.int32)
    far_index = jnp.arange(NBLK, dtype=jnp.int32)

    def one_block(block_id):
        first_row = (block_id * SEGMENT_LENGTH).astype(jnp.int32)
        request_vectors = lax.dynamic_slice_in_dim(queries, first_row, SEGMENT_LENGTH, 1).astype(jnp.float32).reshape(SEQS, SEGMENT_LENGTH, HEADS, CHANNEL_WIDTH)
        address_vectors = lax.dynamic_slice_in_dim(keys_padded, first_row, 2 * SEGMENT_LENGTH, 1).astype(jnp.float32).reshape(SEQS, 2 * SEGMENT_LENGTH, HEADS, CHANNEL_WIDTH)
        value_rows = lax.dynamic_slice_in_dim(values_padded, first_row, 2 * SEGMENT_LENGTH, 1).astype(jnp.float32).reshape(SEQS, 2 * SEGMENT_LENGTH, HEADS, CHANNEL_WIDTH)
        adjacent_similarity = jnp.einsum('zplr,zblr->zlpb', request_vectors, address_vectors) * softmax_multiplier
        within_block = (key_pos[None, :] >= SEGMENT_LENGTH) & (key_pos[None, :] - SEGMENT_LENGTH <= query_pos[:, None])
        preceding_segment = (key_pos[None, :] < SEGMENT_LENGTH) & (block_id >= 1)
        adjacent_similarity = jnp.where((within_block | preceding_segment)[None, None], adjacent_similarity, -jnp.inf)
        faraway_similarity = jnp.einsum('fwqo,fxqo->fqwx', request_vectors, span_address_means) * softmax_multiplier + faraway_offset_bias
        faraway_similarity = jnp.where((far_index < block_id - 1)[None, None, None, :], faraway_similarity, -jnp.inf)
        row_max = jnp.maximum(lax.optimization_barrier(jnp.max(adjacent_similarity, axis=-1)), lax.optimization_barrier(jnp.max(faraway_similarity, axis=-1)))[..., None]
        near_w = jnp.exp(adjacent_similarity - row_max)
        far_w = jnp.exp(faraway_similarity - row_max)
        row_total = lax.optimization_barrier(jnp.sum(near_w, axis=-1, keepdims=True)) + lax.optimization_barrier(jnp.sum(far_w, axis=-1, keepdims=True))
        near_p = lax.optimization_barrier((near_w / row_total).astype(jnp.bfloat16)).astype(jnp.float32)
        far_p = lax.optimization_barrier((far_w / row_total).astype(jnp.bfloat16)).astype(jnp.float32)
        attended = jnp.einsum('shqk,skhd->sqhd', near_p, value_rows) + jnp.einsum('shqj,sjhd->sqhd', far_p, value_means)
        attended = attended.astype(jnp.bfloat16).reshape(SEQS * SEGMENT_LENGTH, feature_width)
        result = jnp.dot(attended, out_weight, preferred_element_type=jnp.float32).astype(jnp.bfloat16)
        return result.reshape(SEQS, SEGMENT_LENGTH, D)
    segment_outcomes = lax.map(one_block, jnp.arange(NBLK, dtype=jnp.int32))
    return jnp.transpose(segment_outcomes, (1, 0, 2, 3)).reshape(SEQS, LENGTH, D)
```

```python
import math

import jax
import jax.numpy as jnp
from jax import lax
from jax.experimental import pallas as pl
from jax.experimental.pallas import tpu as pltpu
from jax.sharding import PartitionSpec as P

HEAD = 128
BLOCK = 256
SCALE = math.log2(math.e) / math.sqrt(HEAD)
FAR_BIAS = math.log(BLOCK) * math.sqrt(HEAD)
LOW = -1e30
SIDE = 4

BF16 = jnp.bfloat16
F32 = jnp.float32


def split_place(s):
    return s // (2 * SIDE), (s // 2) % SIDE, s % 2


def join_place(x, y, c):
    return ((x % SIDE) * SIDE + y % SIDE) * 2 + c


def move(value, dx, dy, flip=0):
    count = lax.axis_size("seq")
    pairs = []
    for s in range(count):
        x, y, c = split_place(s)
        pairs.append((s, join_place(x + dx, y + dy, c ^ flip)))
    return lax.ppermute(value, "seq", pairs)


def ring(value, step):
    count = lax.axis_size("dp")
    return lax.ppermute(value, "dp", [(z, (z + step) % count) for z in range(count)])


def shifted(value):
    count = lax.axis_size("seq")
    return lax.ppermute(value, "seq", [(s, s + 1) for s in range(count - 1)])


def attention_block(info, q_ref, kp_ref, ko_ref, vp_ref, vo_ref, fk_ref, fv_ref, o_ref, local, heads):
    block = info[0] + local
    row = lax.broadcasted_iota(jnp.int32, (BLOCK, BLOCK), 0)
    col = lax.broadcasted_iota(jnp.int32, (BLOCK, BLOCK), 1)
    causal = col <= row
    far_count = fk_ref.shape[0]
    far_seen = lax.broadcasted_iota(jnp.int32, (BLOCK, far_count), 1) < block - 1
    contract = (((1,), (1,)), ((), ()))
    for h in range(heads):
        lanes = slice(h * HEAD, (h + 1) * HEAD)
        q = q_ref[:, lanes]
        s_prev = lax.dot_general(q, kp_ref[:, lanes], contract, preferred_element_type=F32)
        s_own = lax.dot_general(q, ko_ref[:, lanes], contract, preferred_element_type=F32)
        s_far = lax.dot_general(q, fk_ref[:, lanes], contract, preferred_element_type=F32)
        if local == 0:
            s_prev = jnp.where(block > 0, s_prev, LOW)
        s_own = jnp.where(causal, s_own, LOW)
        s_far = jnp.where(far_seen, s_far + FAR_BIAS, LOW)
        top = jnp.maximum(
            jnp.max(jnp.maximum(s_prev, s_own), axis=1, keepdims=True),
            jnp.max(s_far, axis=1, keepdims=True),
        )
        p_prev = jnp.exp2((s_prev - top) * SCALE)
        p_own = jnp.exp2((s_own - top) * SCALE)
        p_far = jnp.exp2((s_far - top) * SCALE)
        total = jnp.sum(p_prev + p_own, axis=1, keepdims=True) + jnp.sum(p_far, axis=1, keepdims=True)
        out = jnp.dot(p_prev.astype(BF16), vp_ref[:, lanes], preferred_element_type=F32)
        out += jnp.dot(p_own.astype(BF16), vo_ref[:, lanes], preferred_element_type=F32)
        out += jnp.dot(p_far.astype(BF16), fv_ref[:, lanes], preferred_element_type=F32)
        o_ref[:, lanes] = (out * (1.0 / total)).astype(BF16)


HEADS_PER_STEP = 4


def attend(info, local, q, kp, ko, vp, vo, fk, fv, earlier=None):
    rows, width = q.shape
    wide = HEADS_PER_STEP * HEAD

    def spec(at):
        return pl.BlockSpec((BLOCK, wide), lambda g, info: (at, g))

    far_spec = pl.BlockSpec((fk.shape[0], wide), lambda g, info: (0, g))
    args = [q, kp[0], ko[0], vp[0], vo[0], fk, fv]
    specs = [spec(local), spec(kp[1]), spec(ko[1]), spec(vp[1]), spec(vo[1]), far_spec, far_spec]
    aliases = {}
    if earlier is not None:
        aliases = {1 + len(args): 0}
        args.append(earlier)
        specs.append(pl.BlockSpec(memory_space=pl.ANY))

    def kernel(info, *refs):
        attention_block(info, *refs[:7], refs[-1], local, HEADS_PER_STEP)

    near = 2 * BLOCK + fk.shape[0]
    return pl.pallas_call(
        kernel,
        out_shape=jax.ShapeDtypeStruct((rows, width), BF16),
        grid_spec=pltpu.PrefetchScalarGridSpec(
            num_scalar_prefetch=1,
            grid=(width // wide,),
            in_specs=specs,
            out_specs=spec(local),
        ),
        input_output_aliases=aliases,
        cost_estimate=pl.CostEstimate(
            flops=4 * BLOCK * near * width,
            bytes_accessed=2 * width * (6 * BLOCK + 2 * fk.shape[0]),
            transcendentals=BLOCK * near * (width // HEAD),
        ),
        compiler_params=pltpu.CompilerParams(vmem_limit_bytes=40 << 20),
        name=f"attend_{local}",
    )(info, *args)


HALF = 256


def project(table, own, partner, pieces, shards, arrived, out, whole=None):
    rows, depth = own.shape
    copies = 0 if arrived is None else arrived.shape[0]
    steps = shards + copies
    last = shards - 1
    full = pl.BlockSpec((rows, depth), lambda s, t: (0, 0))
    args = [own, partner]
    specs = [full, full]
    if whole is not None:
        args.append(whole)
        specs.append(pl.BlockSpec((depth, HALF), lambda s, t: (0, t[0])))
        sources = 1
    else:
        sources = len(pieces)
        for piece in pieces:
            args.append(piece)
            specs.append(pl.BlockSpec((piece.shape[0] // shards, HALF), lambda s, t: (jnp.minimum(s, last), 0)))
    if copies:
        args.append(arrived)
        specs.append(pl.BlockSpec((None, rows, HALF), lambda s, t: (jnp.maximum(s - shards, 0), 0, 0)))
    aliases = {}
    if out is not None:
        aliases = {1 + len(args): 0}
        args.append(out)
        specs.append(pl.BlockSpec(memory_space=pl.ANY))

    def kernel(t, own_ref, partner_ref, *refs):
        weights = refs[:sources]
        out_ref, send_ref = refs[-2], refs[-1]

        def compute():
            for lhs, dst in ((partner_ref, send_ref), (own_ref, out_ref)):
                if whole is not None:
                    acc = jnp.dot(lhs[...], weights[0][...], preferred_element_type=F32)
                else:
                    acc = None
                    for i, weight in enumerate(weights):
                        part = weight.shape[0]
                        at = pl.multiple_of(((t[0] + i) % sources) * part, part)
                        term = jnp.dot(lhs[:, pl.ds(at, part)], weight[...], preferred_element_type=F32)
                        acc = term if acc is None else acc + term
                dst[...] = acc.astype(BF16)

        if copies:
            pl.when(pl.program_id(0) < shards)(compute)

            @pl.when(pl.program_id(0) >= shards)
            def _():
                out_ref[...] = refs[sources][...]
        else:
            compute()

    return pl.pallas_call(
        kernel,
        out_shape=(
            jax.ShapeDtypeStruct((1, rows, 16 * HALF), BF16),
            jax.ShapeDtypeStruct((shards, rows, HALF), BF16),
        ),
        grid_spec=pltpu.PrefetchScalarGridSpec(
            num_scalar_prefetch=1,
            grid=(steps,),
            in_specs=specs,
            out_specs=(
                pl.BlockSpec((None, rows, HALF), lambda s, t: (0, 0, t[1 + s])),
                pl.BlockSpec((None, rows, HALF), lambda s, t: (jnp.minimum(s, last), 0, 0)),
            ),
        ),
        input_output_aliases=aliases,
        cost_estimate=pl.CostEstimate(
            flops=4 * rows * depth * HALF * shards,
            bytes_accessed=4 * rows * depth + 2 * shards * HALF * (depth + 2 * rows),
            transcendentals=0,
        ),
        compiler_params=pltpu.CompilerParams(vmem_limit_bytes=50 << 20),
        name=f"project_{shards}_{copies}_{sources}",
    )(table, *args)


def place(table, arrived, out):
    copies, rows, _ = arrived.shape

    def kernel(t, in_ref, _, out_ref):
        out_ref[...] = in_ref[...]

    return pl.pallas_call(
        kernel,
        out_shape=jax.ShapeDtypeStruct(out.shape, BF16),
        grid_spec=pltpu.PrefetchScalarGridSpec(
            num_scalar_prefetch=1,
            grid=(copies,),
            in_specs=[
                pl.BlockSpec((None, rows, HALF), lambda s, t: (s, 0, 0)),
                pl.BlockSpec(memory_space=pl.ANY),
            ],
            out_specs=pl.BlockSpec((None, rows, HALF), lambda s, t: (0, 0, t[s])),
        ),
        input_output_aliases={2: 0},
        name="place",
    )(table, arrived, out)


def per_device(queries, keys, values, out_weight):
    rows, width = queries.shape[1:]
    blocks = rows // BLOCK
    shards = lax.axis_size("seq")
    s = lax.axis_index("seq")
    z = lax.axis_index("dp")
    nz = lax.axis_size("dp")
    x, y, c = split_place(s)
    color = (x + 2 * y) % 4
    q, k, v = queries[0], keys[0], values[0]
    depth = out_weight.shape[0]
    part = depth // 4

    mine = lax.dynamic_slice(out_weight, (color * part, c * HALF), (part, HALF))
    down, up = [mine], [mine]
    for step in (1, 2, 3):
        down.append(ring(down[-1], 1))
        up.append(ring(up[-1], -1))
    far_down = ring(down[3][: part // 2], 1)
    far_up = ring(up[3][part // 2 :], -1)
    gathered = []
    for step in (1, 2, 3, 4):
        if step < 4:
            pair = jnp.concatenate([down[step], up[step]], axis=0)
        else:
            pair = jnp.concatenate([far_down, far_up], axis=0)
        gathered.append((pair, move(pair, -1, 0), move(pair, 0, -1), move(pair, 1, 0)))

    prev_k = shifted(k[rows - BLOCK :])
    prev_v = shifted(v[rows - BLOCK :])
    means = [
        jnp.mean(a.reshape(blocks, BLOCK, width), axis=1, dtype=F32).astype(BF16) for a in (k, v)
    ]
    packed = jnp.broadcast_to(jnp.concatenate(means, axis=0)[None], (shards, 2 * blocks, width))
    spread = lax.all_to_all(packed, "seq", 0, 0)
    far_k = spread[:, :blocks].reshape(shards * blocks, width)
    far_v = spread[:, blocks:].reshape(shards * blocks, width)

    info = jnp.stack([s * blocks]).astype(jnp.int32)
    att = attend(info, 1, q, (k, 0), (k, 1), (v, 0), (v, 1), far_k, far_v)
    att = attend(info, 0, q, (prev_k, 0), (k, 0), (prev_v, 0), (v, 0), far_k, far_v, att)
    partner = move(att, 0, 0, 1)

    def cols(steps, side):
        return [((z + d) % nz) * 2 + (c if side else 1 - c) for d in steps]

    def table(*entries):
        return jnp.stack([jnp.asarray(e, jnp.int32) for e in entries])

    out, send = project(table(c, *cols([0], True)), att, partner, None, 1, None, None, whole=out_weight)
    arrived, before = move(send, 0, 0, 1), [0]
    for step in (1, 2, 3, 4):
        now = [-step, step] if step < 4 else [4]
        out, send = project(
            table(color, *cols(now, True), *cols(before, False)),
            att, partner, gathered[step - 1], len(now), arrived, out,
        )
        arrived, before = move(send, 0, 0, 1), now
    return place(table(*cols(before, False)), arrived, out)


def solution(mesh):
    return jax.shard_map(
        per_device,
        mesh=mesh,
        in_specs=(P("dp", "seq", None), P("dp", "seq", None), P("dp", "seq", None), P(None, "dp")),
        out_specs=P("dp", "seq", None),
        check_vma=False,
    )
```
